32 devices in a mesh: groups: 2 (over x), row: 16 (over z, y, core).
Axes of the slice: x: 2, y: 2, z: 4, core: 2. Of those that a mesh axis runs over, the one named last changes fastest.
Arguments:
- bound_coeff: bfloat16 [4, 64, 8192], P('groups', 'row'), parts along dimension 0, may hold values from -0.044 to 0.044
- status: int32 [4, 8192], P('groups'), parts along dimension 0, may hold values from 0 to 2
- slope_bit: int32 [4, 8192], P('groups'), parts along dimension 0, may hold values from 0 to 1
- pre_lower: float32 [4, 8192], P('groups'), parts along dimension 0, may hold values from -2 to -0.1
- pre_upper: float32 [4, 8192], P('groups'), parts along dimension 0, may hold values from 0.1 to 2
- weight: bfloat16 [16384, 8192], P('groups', 'row'), parts along dimension 0, may hold values from -0.0625 to 0.0625
- layer_bias: float32 [16384], P('groups'), parts along dimension 0, may hold values from -6 to 6
- center_input: float32 [4, 8192], P('groups', 'row'), parts along dimension 0, may hold values from -6 to 6
- radius: float32 [4, 8192], P('groups', 'row'), parts along dimension 0, may hold values from 0.05 to 1
Outputs:
- lower_bound: float32 [4, 64], P('groups', 'row'), parts along dimension 0
- upper_bound: float32 [4, 64], P('groups', 'row'), parts along dimension 0
The draws below stay inside these ranges and needn't reach their ends.
There are 2 independent parts, one for each index of `groups`. The reference program is written for one: setup_inputs(seed, part) draws one part's arguments, and reference() takes and returns one part's arrays. A program takes and returns all parts, laid end to end along the dimension named above; each array names one. Nothing has to cross between parts.
All inputs are finite; a program needn't handle non-finite values.
Results may differ from the reference program's by a relative error of at most 0.0003.
Values may be sent and summed in bfloat16 or wider, within the bound.
No kernel may reach another device: no remote copies, remote signals or barrier semaphores. Data moves between devices by JAX's collectives and lax.ppermute only.
A program may use at most 64 MiB of HBM per device.

```python
import math
import jax
import jax.numpy as jnp
from jax import lax

EX = 2
H = 8192
D = 8192
SPECS = 64


def draw_bound_coeff(key, part):
    scale_key, value_key = jax.random.split(key)
    row_scale = jnp.exp(jax.random.uniform(scale_key, (EX, SPECS, 1), jnp.float32, math.log(0.1), math.log(1.0)))
    values = jax.random.truncated_normal(value_key, -4.0, 4.0, (EX, SPECS, H), jnp.float32)
    return (values * row_scale * 0.011).astype(jnp.bfloat16)


def draw_radius(key, part):
    coarse_key, fine_key = jax.random.split(key)
    blocks = D // 128
    coarse = jnp.exp(jax.random.uniform(coarse_key, (EX, blocks, 1), jnp.float32, math.log(0.1), math.log(1.0)))
    fine = jnp.exp(jax.random.uniform(fine_key, (EX, blocks, 128), jnp.float32, math.log(0.5), math.log(1.0)))
    return (coarse * fine).reshape(EX, D)


def touch_ends(entries, stream_key, low, high):
    spot = [jax.random.randint(jax.random.fold_in(stream_key, axis), (), 0, length) for axis, length in enumerate(entries.shape)]
    longest = entries.shape.index(max(entries.shape))
    neighbour = spot[:longest] + [(spot[longest] + 1) % entries.shape[longest]] + spot[longest + 1:]
    return entries.at[tuple(spot)].set(low).at[tuple(neighbour)].set(high)


def block_scale(rng, extent, cuts, low, high):
    loudness, own = 1.0, jax.random.fold_in(rng, 6)
    for position, parts in cuts:
        heights = jnp.exp(jax.random.uniform(jax.random.fold_in(own, position), (parts,), jnp.float32, low / len(cuts), high / len(cuts)))
        loudness = loudness * jnp.repeat(heights, extent[position] // parts).reshape([-1 if axis == position else 1 for axis in range(len(extent))])
    return loudness


def noise(stream_key, shape, deviation, bound, pieces=(), held_as=jnp.bfloat16):
    entries = jax.random.normal(stream_key, shape, jnp.float32) * deviation
    if len(pieces) > 0:
        entries = block_scale(stream_key, shape, pieces, -0.22, 0.18) * entries
    return jnp.clip(entries, min=-bound, max=bound).astype(held_as)


def setup_inputs(seed: int = 0, part: int = 0) -> dict:
    keys = jax.random.split(jax.random.key(seed), 10)
    own_keys = jax.random.split(jax.random.fold_in(keys[9], part), 10)
    return {
        "bound_coeff": draw_bound_coeff(jax.random.fold_in(jax.random.fold_in(keys[9], part), 71), part),
        "status": touch_ends(jax.random.randint(own_keys[1], (EX, H), 0, 3), jax.random.fold_in(own_keys[1], 1), 0, 2).astype(jnp.int32),
        "slope_bit": touch_ends(jax.random.randint(own_keys[2], (EX, H), 0, 2), jax.random.fold_in(own_keys[2], 1), 0, 1).astype(jnp.int32),
        "pre_lower": jnp.clip(jax.random.uniform(own_keys[3], (EX, H), jnp.float32, -2.0, -0.1), -2.0, -0.1),
        "pre_upper": jnp.clip(jax.random.uniform(own_keys[4], (EX, H), jnp.float32, 0.1, 2.0), 0.1, 2.0),
        "weight": noise(own_keys[5], (H, D), D ** -0.5, 0.0625, ((1, 16),)),
        "layer_bias": noise(own_keys[6], (H,), 1.0, 6.0, (), jnp.float32),
        "center_input": noise(own_keys[7], (EX, D), 1.0, 6.0, ((1, 16),), jnp.float32),
        "radius": draw_radius(jax.random.fold_in(jax.random.fold_in(keys[9], part), 71), part),
    }


def relax_coeff(bound_coeff, status, slope_bit, pre_lower, pre_upper):
    values = bound_coeff.astype(jnp.float32)
    upper_slope = (pre_upper / (pre_upper - pre_lower))[:, None, :]
    chosen = slope_bit.astype(jnp.float32)[:, None, :]
    unstable = (status == 2)[:, None, :]
    active = (status == 1)[:, None, :]
    positive = values >= 0.0
    slope_low = jnp.where(active, 1.0, jnp.where(unstable, jnp.where(positive, chosen, upper_slope), 0.0))
    slope_up = jnp.where(active, 1.0, jnp.where(unstable, jnp.where(positive, upper_slope, chosen), 0.0))
    return (values * slope_low).astype(jnp.bfloat16), (values * slope_up).astype(jnp.bfloat16)


def intercepts(bound_coeff, status, pre_lower, pre_upper):
    values = bound_coeff.astype(jnp.float32)
    upper_slope = pre_upper / (pre_upper - pre_lower)
    offset = (-upper_slope * pre_lower)[:, None, :]
    unstable = (status == 2)[:, None, :]
    positive = values >= 0.0
    below_term = jnp.sum(jnp.where(unstable & jnp.logical_not(positive), values * offset, 0.0), axis=-1)
    above_term = jnp.sum(jnp.where(unstable & positive, values * offset, 0.0), axis=-1)
    return below_term, above_term


def reference(bound_coeff, status, slope_bit, pre_lower, pre_upper, weight, layer_bias, center_input, radius):
    relaxed_low, relaxed_up = relax_coeff(bound_coeff, status, slope_bit, pre_lower, pre_upper)
    below_term, above_term = intercepts(bound_coeff, status, pre_lower, pre_upper)
    center = jnp.einsum("jd,ed->ej", weight.astype(jnp.float32), center_input, precision=lax.Precision.HIGHEST) + layer_bias[None, :]
    near_low = jnp.einsum("erj,ej->er", relaxed_low.astype(jnp.float32), center, precision=lax.Precision.HIGHEST)
    near_up = jnp.einsum("erj,ej->er", relaxed_up.astype(jnp.float32), center, precision=lax.Precision.HIGHEST)
    mapped_low = jnp.dot(relaxed_low.reshape(EX * SPECS, H), weight, preferred_element_type=jnp.float32).reshape(EX, SPECS, D)
    spread_low = jnp.einsum("erd,ed->er", jnp.abs(mapped_low), radius, precision=lax.Precision.HIGHEST)
    mapped_up = jnp.dot(relaxed_up.reshape(EX * SPECS, H), weight, preferred_element_type=jnp.float32).reshape(EX, SPECS, D)
    spread_up = jnp.einsum("erd,ed->er", jnp.abs(mapped_up), radius, precision=lax.Precision.HIGHEST)
    lower_bound = near_low + below_term - spread_low
    upper_bound = near_up + above_term + spread_up
    return (lower_bound, upper_bound)
```

```python
import jax
import jax.numpy as jnp
from jax import lax
from jax.sharding import PartitionSpec as P


def slopes(status, slope_bit, pre_lower, pre_upper):
    upper_slope = pre_upper / (pre_upper - pre_lower)
    chosen = slope_bit.astype(jnp.float32)
    unstable = status == 2
    active = status == 1
    inner = jnp.where(active, 1.0, jnp.where(unstable, chosen, 0.0))
    outer = jnp.where(active, 1.0, jnp.where(unstable, upper_slope, 0.0))
    offset = jnp.where(unstable, -upper_slope * pre_lower, 0.0)
    return inner, outer, offset


def relax(values, inner, outer):
    positive = values >= 0.0
    low = values * jnp.where(positive, inner, outer)
    up = values * jnp.where(positive, outer, inner)
    return low.astype(jnp.bfloat16), up.astype(jnp.bfloat16)


def on_device(
    bound_coeff, status, slope_bit, pre_lower, pre_upper, weight, layer_bias, center_input, radius
):
    examples = bound_coeff.shape[0]
    num_neurons = bound_coeff.shape[2]
    local_cols = weight.shape[1]
    inner, outer, offset = slopes(status, slope_bit, pre_lower, pre_upper)
    inner, outer, offset = inner[:, None, :], outer[:, None, :], offset[:, None, :]

    values = bound_coeff.astype(jnp.float32)
    own_low, own_up = relax(values, inner, outer)
    term = values * offset
    bias = layer_bias[None, None, :]
    own_lower = jnp.sum(jnp.where(values < 0.0, term, 0.0) + own_low.astype(jnp.float32) * bias, axis=-1)
    own_upper = jnp.sum(jnp.where(values >= 0.0, term, 0.0) + own_up.astype(jnp.float32) * bias, axis=-1)

    gathered = lax.all_gather(bound_coeff, "row", axis=0, tiled=False)
    num_devices = gathered.shape[0]
    low, up = relax(gathered.astype(jnp.float32), inner, outer)
    stacked = jnp.stack([low, up], axis=1)
    mapped = jnp.dot(
        stacked.reshape(-1, num_neurons), weight, preferred_element_type=jnp.float32
    ).reshape(num_devices, 2, examples, -1, local_cols)
    sign = jnp.array([-1.0, 1.0], dtype=jnp.float32)[None, :, None, None, None]
    cell = mapped * center_input[None, None, :, None, :] + sign * jnp.abs(mapped) * radius[None, None, :, None, :]
    part = jnp.sum(cell, axis=-1)
    mine = jnp.sum(lax.all_to_all(part, "row", 0, 0, tiled=True), axis=0)
    return (own_lower + mine[0], own_upper + mine[1])


def solution(mesh):
    in_specs = (
        P("groups", "row", None),
        P("groups", None),
        P("groups", None),
        P("groups", None),
        P("groups", None),
        P("groups", "row"),
        P("groups"),
        P("groups", "row"),
        P("groups", "row"),
    )
    out_specs = (P("groups", "row"), P("groups", "row"))
    return jax.shard_map(
        on_device, mesh=mesh, in_specs=in_specs, out_specs=out_specs, check_vma=False
    )
```

```python
import functools

import jax
import jax.numpy as jnp
from jax import lax
from jax.experimental import pallas as pl
from jax.experimental.pallas import tpu as pltpu
from jax.sharding import PartitionSpec as P

F32 = jnp.float32
BF16 = jnp.bfloat16
LANES = 128
VMEM = pl.BlockSpec(memory_space=pltpu.VMEM)


def lane_sums(cells):
    rows, columns = cells.shape
    width = min(columns, LANES)
    folded = cells[:, 0:width]
    for start in range(width, columns, width):
        folded = folded + cells[:, start : start + width]
    return jnp.sum(folded.T, axis=0, keepdims=True)


def prep_kernel(coeff, status, bit, lower, upper, bias, inner_out, outer_out, own_out):
    examples, specs, neurons = coeff.shape
    low, high = lower[...], upper[...]
    slope = high / (high - low)
    unstable = status[...] == 2
    active = status[...] == 1
    inner = jnp.where(active, 1.0, jnp.where(unstable, bit[...].astype(F32), 0.0))
    outer = jnp.where(active, 1.0, jnp.where(unstable, slope, 0.0))
    offset = jnp.where(unstable, -slope * low, 0.0)
    biases = bias[...]
    below, above = [], []
    for e in range(examples):
        inner_rows = jnp.broadcast_to(inner[e : e + 1], (specs, neurons))
        outer_rows = jnp.broadcast_to(outer[e : e + 1], (specs, neurons))
        inner_out[e * specs : (e + 1) * specs, :] = inner_rows
        outer_out[e * specs : (e + 1) * specs, :] = outer_rows
        values = coeff[e].astype(F32)
        positive = values >= 0.0
        relaxed_low = (values * jnp.where(positive, inner_rows, outer_rows)).astype(BF16).astype(F32)
        relaxed_up = (values * jnp.where(positive, outer_rows, inner_rows)).astype(BF16).astype(F32)
        term = values * offset[e : e + 1]
        below.append(jnp.where(positive, 0.0, term) + relaxed_low * biases)
        above.append(jnp.where(positive, term, 0.0) + relaxed_up * biases)
    cells = jnp.concatenate(below + above, axis=0)
    rows = cells.shape[0]
    folded = cells[:, 0:LANES]
    for start in range(LANES, neurons, LANES):
        folded = folded + cells[:, start : start + LANES]
    if rows < LANES:
        folded = jnp.concatenate([folded, jnp.zeros((LANES - rows, LANES), F32)], axis=0)
    own_out[...] = jnp.sum(folded.T, axis=0, keepdims=True)[:, 0:rows]


def prep(coeff, status, bit, lower, upper, bias):
    examples, specs, neurons = coeff.shape
    rows = examples * specs
    return pl.pallas_call(
        prep_kernel,
        in_specs=[VMEM] * 6,
        out_specs=(VMEM, VMEM, VMEM),
        out_shape=(
            jax.ShapeDtypeStruct((rows, neurons), F32),
            jax.ShapeDtypeStruct((rows, neurons), F32),
            jax.ShapeDtypeStruct((1, 2 * rows), F32),
        ),
        compiler_params=pltpu.CompilerParams(vmem_limit_bytes=16 << 20),
        name="prep",
    )(coeff, status, bit, lower, upper, bias)


def map_kernel(num_pieces, *refs):
    pieces = refs[:num_pieces]
    inner, outer, weight, center, radius, out, relaxed = refs[num_pieces:]
    examples, specs, neurons = pieces[0].shape
    rows = examples * specs
    columns = weight.shape[1]
    step = min(neurons, 2048)
    for start in range(0, neurons, step):
        span = slice(start, start + step)
        inner_rows, outer_rows = inner[:, span], outer[:, span]
        for index, piece in enumerate(pieces):
            values = jnp.concatenate([piece[e, :, span].astype(F32) for e in range(examples)], axis=0)
            positive = values >= 0.0
            low = (values * jnp.where(positive, inner_rows, outer_rows)).astype(BF16)
            up = (values * jnp.where(positive, outer_rows, inner_rows)).astype(BF16)
            at = index * 2 * rows
            relaxed[at : at + 2 * rows, span] = jnp.concatenate([low, up], axis=0)
    mapped = jnp.dot(relaxed[...], weight[...], preferred_element_type=F32)
    centers, radii = center[...], radius[...]

    def per_row(values_low, values_up):
        halves = []
        for values in (values_low, values_up):
            for e in range(examples):
                halves.append(jnp.broadcast_to(values[e : e + 1], (specs, columns)))
        block = jnp.concatenate(halves, axis=0)[None]
        return jnp.broadcast_to(block, (num_pieces, 2 * rows, columns)).reshape(num_pieces * 2 * rows, columns)

    cells = mapped * per_row(centers, centers) + jnp.abs(mapped) * per_row(-radii, radii)
    out[...] = lane_sums(cells)


def map_rows(pieces, inner, outer, weight, center, radius):
    examples, specs, neurons = pieces[0].shape
    rows = 2 * examples * specs * len(pieces)
    columns = weight.shape[1]
    return pl.pallas_call(
        functools.partial(map_kernel, len(pieces)),
        in_specs=[VMEM] * (len(pieces) + 5),
        out_specs=VMEM,
        out_shape=jax.ShapeDtypeStruct((1, rows), F32),
        scratch_shapes=[pltpu.VMEM((rows, neurons), BF16)],
        compiler_params=pltpu.CompilerParams(vmem_limit_bytes=32 << 20),
        cost_estimate=pl.CostEstimate(
            flops=2 * rows * neurons * columns, bytes_accessed=2 * rows * neurons, transcendentals=0
        ),
        name="map_rows",
    )(*pieces, inner, outer, weight, center, radius)


def fold_kernel(kept, came, keep_out, send_out):
    total = kept[...] + came[...]
    half = total.shape[1] // 2
    keep_out[...] = total[:, 0:half]
    send_out[...] = total[:, half:]


def fold(kept, came):
    half = kept.shape[1] // 2
    return pl.pallas_call(
        fold_kernel,
        in_specs=[VMEM] * 2,
        out_specs=(VMEM, VMEM),
        out_shape=(jax.ShapeDtypeStruct((1, half), F32),) * 2,
        name="fold",
    )(kept, came)


def finish_kernel(kept, came, own, lower_out, upper_out):
    total = kept[...] + came[...] + own[...]
    examples, specs = lower_out.shape
    for e in range(examples):
        lower_out[e : e + 1, :] = total[:, e * specs : (e + 1) * specs]
        at = (examples + e) * specs
        upper_out[e : e + 1, :] = total[:, at : at + specs]


def finish(kept, came, own, examples, specs):
    return pl.pallas_call(
        finish_kernel,
        in_specs=[VMEM] * 3,
        out_specs=(VMEM, VMEM),
        out_shape=(jax.ShapeDtypeStruct((examples, specs), F32),) * 2,
        name="finish",
    )(kept, came, own)


def on_device(
    num_devices, bound_coeff, status, slope_bit, pre_lower, pre_upper, weight, layer_bias, center_input, radius
):
    examples, specs, neurons = bound_coeff.shape

    def swap(array, mask):
        return lax.ppermute(array, "row", [(i, i ^ mask) for i in range(num_devices)])

    inner, outer, own = prep(bound_coeff, status, slope_bit, pre_lower, pre_upper, layer_bias.reshape(1, neurons))

    pieces = {0: bound_coeff}
    for mask in range(4, num_devices, 4):
        pieces[mask] = swap(bound_coeff, mask)
    for mask in range(0, num_devices, 4):
        pieces[mask + 2] = swap(pieces[mask], 2)
    for mask in range(0, num_devices, 2):
        pieces[mask + 1] = swap(pieces[mask], 1)

    args = (inner, outer, weight, center_input, radius)
    bits = num_devices.bit_length() - 1
    order = [int(format(i, "b").zfill(bits)[::-1], 2) for i in range(num_devices)]
    half = num_devices // 2
    keep = map_rows([pieces[m] for m in order[:half]], *args)
    send = map_rows([pieces[m] for m in order[half:]], *args)
    for bit in range(bits):
        came = swap(send, 1 << bit)
        if bit < bits - 1:
            keep, send = fold(keep, came)
    return finish(keep, came, own, examples, specs)


def solution(mesh):
    in_specs = (
        P("groups", "row", None),
        P("groups", None),
        P("groups", None),
        P("groups", None),
        P("groups", None),
        P("groups", "row"),
        P("groups"),
        P("groups", "row"),
        P("groups", "row"),
    )
    out_specs = (P("groups", "row"), P("groups", "row"))
    return jax.shard_map(
        functools.partial(on_device, mesh.shape["row"]),
        mesh=mesh,
        in_specs=in_specs,
        out_specs=out_specs,
        check_vma=False,
    )
```

```python
import functools

import jax
import jax.numpy as jnp
from jax import lax
from jax.experimental import pallas as pl
from jax.experimental.pallas import tpu as pltpu
from jax.sharding import PartitionSpec as P

F32 = jnp.float32
BF16 = jnp.bfloat16
LANES = 128
VMEM = pl.BlockSpec(memory_space=pltpu.VMEM)


def lane_sums(cells):
    rows, columns = cells.shape
    width = min(columns, LANES)
    folded = cells[:, 0:width]
    for start in range(width, columns, width):
        folded = folded + cells[:, start : start + width]
    return jnp.sum(folded.T, axis=0, keepdims=True)


def prep_kernel(*refs):
    sources, (inner_out, outer_out, own_out, weight_out), held, done = refs[:7], refs[7:11], refs[11:17], refs[17]
    targets = (*held, weight_out)
    copies = [pltpu.make_async_copy(s, t, done.at[i]) for i, (s, t) in enumerate(zip(sources, targets))]
    for copy in copies:
        copy.start()
    for copy in copies[:-1]:
        copy.wait()
    coeff, status, bit, lower, upper, bias = held
    examples, specs, neurons = coeff.shape
    low, high = lower[...], upper[...]
    slope = high / (high - low)
    unstable = status[...] == 2
    active = status[...] == 1
    inner = jnp.where(active, 1.0, jnp.where(unstable, bit[...].astype(F32), 0.0))
    outer = jnp.where(active, 1.0, jnp.where(unstable, slope, 0.0))
    offset = jnp.where(unstable, -slope * low, 0.0)
    biases = bias[...]
    below, above = [], []
    for e in range(examples):
        inner_rows = jnp.broadcast_to(inner[e : e + 1], (specs, neurons))
        outer_rows = jnp.broadcast_to(outer[e : e + 1], (specs, neurons))
        inner_out[e * specs : (e + 1) * specs, :] = inner_rows
        outer_out[e * specs : (e + 1) * specs, :] = outer_rows
        values = coeff[e].astype(F32)
        positive = values >= 0.0
        relaxed_low = (values * jnp.where(positive, inner_rows, outer_rows)).astype(BF16).astype(F32)
        relaxed_up = (values * jnp.where(positive, outer_rows, inner_rows)).astype(BF16).astype(F32)
        term = values * offset[e : e + 1]
        below.append(jnp.where(positive, 0.0, term) + relaxed_low * biases)
        above.append(jnp.where(positive, term, 0.0) + relaxed_up * biases)
    cells = jnp.concatenate(below + above, axis=0)
    rows = cells.shape[0]
    folded = cells[:, 0:LANES]
    for start in range(LANES, neurons, LANES):
        folded = folded + cells[:, start : start + LANES]
    if rows < LANES:
        folded = jnp.concatenate([folded, jnp.zeros((LANES - rows, LANES), F32)], axis=0)
    own_out[...] = jnp.sum(folded.T, axis=0, keepdims=True)[:, 0:rows]
    copies[-1].wait()


def prep(coeff, status, bit, lower, upper, bias, weight):
    examples, specs, neurons = coeff.shape
    rows = examples * specs
    small = (coeff, status, bit, lower, upper, bias)
    return pl.pallas_call(
        prep_kernel,
        in_specs=[pl.BlockSpec(memory_space=pltpu.HBM)] * 7,
        out_specs=(VMEM, VMEM, VMEM, VMEM),
        out_shape=(
            jax.ShapeDtypeStruct((rows, neurons), F32),
            jax.ShapeDtypeStruct((rows, neurons), F32),
            jax.ShapeDtypeStruct((1, 2 * rows), F32),
            jax.ShapeDtypeStruct(weight.shape, weight.dtype),
        ),
        scratch_shapes=[pltpu.VMEM(a.shape, a.dtype) for a in small] + [pltpu.SemaphoreType.DMA((7,))],
        compiler_params=pltpu.CompilerParams(vmem_limit_bytes=8 << 20),
        cost_estimate=pl.CostEstimate(
            flops=20 * rows * neurons, bytes_accessed=2 * weight.size + 12 * rows * neurons, transcendentals=0
        ),
        name="prep",
    )(*[pltpu.with_memory_space_constraint(a, pltpu.HBM) for a in (*small, weight)])


def map_kernel(num_pieces, *refs):
    pieces = refs[:num_pieces]
    inner, outer, weight, center, radius, out, relaxed = refs[num_pieces:]
    examples, specs, neurons = pieces[0].shape
    rows = examples * specs
    columns = weight.shape[1]
    step = min(neurons, 2048)
    for start in range(0, neurons, step):
        span = slice(start, start + step)
        inner_rows, outer_rows = inner[:, span], outer[:, span]
        for index, piece in enumerate(pieces):
            values = jnp.concatenate([piece[e, :, span].astype(F32) for e in range(examples)], axis=0)
            positive = values >= 0.0
            low = (values * jnp.where(positive, inner_rows, outer_rows)).astype(BF16)
            up = (values * jnp.where(positive, outer_rows, inner_rows)).astype(BF16)
            at = index * 2 * rows
            relaxed[at : at + 2 * rows, span] = jnp.concatenate([low, up], axis=0)
    mapped = jnp.dot(relaxed[...], weight[...], preferred_element_type=F32)
    centers, radii = center[...], radius[...]

    def per_row(values_low, values_up):
        halves = []
        for values in (values_low, values_up):
            for e in range(examples):
                halves.append(jnp.broadcast_to(values[e : e + 1], (specs, columns)))
        block = jnp.concatenate(halves, axis=0)[None]
        return jnp.broadcast_to(block, (num_pieces, 2 * rows, columns)).reshape(num_pieces * 2 * rows, columns)

    cells = mapped * per_row(centers, centers) + jnp.abs(mapped) * per_row(-radii, radii)
    out[...] = lane_sums(cells)


def join_kernel(order, num_pieces, *refs):
    *ins, early, keep_out, send_out, relaxed, late = refs
    map_kernel(num_pieces, *ins, late, relaxed)
    width = early.shape[1] // (len(order) - num_pieces)
    parts = []
    for source, index in order:
        parts.append((early, late)[source][:, index * width : (index + 1) * width])
    half = len(parts) // 2
    keep_out[...] = jnp.concatenate(parts[:half], axis=1)
    send_out[...] = jnp.concatenate(parts[half:], axis=1)


def map_rows(pieces, args, early=None, order=None):
    examples, specs, neurons = pieces[0].shape
    rows = 2 * examples * specs * len(pieces)
    columns = args[2].shape[1]
    scratch = [pltpu.VMEM((rows, neurons), BF16)]
    if early is None:
        kernel, more = functools.partial(map_kernel, len(pieces)), ()
        out_specs, out_shape = VMEM, jax.ShapeDtypeStruct((1, rows), F32)
    else:
        kernel, more = functools.partial(join_kernel, order, len(pieces)), (early,)
        half = (rows + early.shape[1]) // 2
        out_specs, out_shape = (VMEM, VMEM), (jax.ShapeDtypeStruct((1, half), F32),) * 2
        scratch.append(pltpu.VMEM((1, rows), F32))
    return pl.pallas_call(
        kernel,
        in_specs=[VMEM] * (len(pieces) + len(args) + len(more)),
        out_specs=out_specs,
        out_shape=out_shape,
        scratch_shapes=scratch,
        compiler_params=pltpu.CompilerParams(vmem_limit_bytes=24 << 20),
        cost_estimate=pl.CostEstimate(
            flops=2 * rows * neurons * columns, bytes_accessed=2 * rows * neurons, transcendentals=0
        ),
        name="map_rows",
    )(*pieces, *args, *more)


def fold_kernel(kept, came, keep_out, send_out):
    total = kept[...] + came[...]
    half = total.shape[1] // 2
    keep_out[...] = total[:, 0:half]
    send_out[...] = total[:, half:]


def fold(kept, came):
    half = kept.shape[1] // 2
    return pl.pallas_call(
        fold_kernel,
        in_specs=[VMEM] * 2,
        out_specs=(VMEM, VMEM),
        out_shape=(jax.ShapeDtypeStruct((1, half), F32),) * 2,
        compiler_params=pltpu.CompilerParams(vmem_limit_bytes=1 << 20),
        name="fold",
    )(kept, came)


def finish_kernel(kept, came, own, lower_out, upper_out):
    total = kept[...] + came[...] + own[...]
    examples, specs = lower_out.shape
    for e in range(examples):
        lower_out[e : e + 1, :] = total[:, e * specs : (e + 1) * specs]
        at = (examples + e) * specs
        upper_out[e : e + 1, :] = total[:, at : at + specs]


def finish(kept, came, own, examples, specs):
    return pl.pallas_call(
        finish_kernel,
        in_specs=[VMEM] * 3,
        out_specs=(VMEM, VMEM),
        out_shape=(jax.ShapeDtypeStruct((examples, specs), F32),) * 2,
        compiler_params=pltpu.CompilerParams(vmem_limit_bytes=1 << 20),
        name="finish",
    )(kept, came, own)


def on_device(
    num_devices, bound_coeff, status, slope_bit, pre_lower, pre_upper, weight, layer_bias, center_input, radius
):
    examples, specs, neurons = bound_coeff.shape

    def swap(array, mask):
        return lax.ppermute(array, "row", [(i, i ^ mask) for i in range(num_devices)])

    inner, outer, own, held = prep(
        bound_coeff, status, slope_bit, pre_lower, pre_upper, layer_bias.reshape(1, neurons), weight
    )

    pieces = {0: bound_coeff}
    for mask in range(4, num_devices, 4):
        pieces[mask] = swap(bound_coeff, mask)
    pieces[4], held = lax.optimization_barrier((pieces[4], held))
    for mask in range(0, num_devices, 4):
        pieces[mask + 2] = swap(pieces[mask], 2)
    args = (inner, outer, held, center_input, radius)
    early = [0, 4, 2, 6, 1, 5, 3, 7]
    late = sorted(set(range(num_devices)) - set(early), key=lambda m: (m & 1, m & 2, -m))
    for mask in (0, 4, 2, 6):
        pieces[mask + 1] = swap(pieces[mask], 1)
    first = map_rows([pieces[m] for m in early], args)
    for mask in late:
        if mask & 1 == 0:
            pieces[mask + 1] = swap(pieces[mask], 1)

    bits = num_devices.bit_length() - 1
    sent = [int(format(i, "b").zfill(bits)[::-1], 2) for i in range(num_devices)]
    order = [(0, early.index(m)) if m in early else (1, late.index(m)) for m in sent]
    keep, send = map_rows([pieces[m] for m in late], args, first, order)
    for bit in range(bits):
        came = swap(send, 1 << bit)
        if bit < bits - 1:
            keep, send = fold(keep, came)
    return finish(keep, came, own, examples, specs)


def solution(mesh):
    in_specs = (
        P("groups", "row", None),
        P("groups", None),
        P("groups", None),
        P("groups", None),
        P("groups", None),
        P("groups", "row"),
        P("groups"),
        P("groups", "row"),
        P("groups", "row"),
    )
    out_specs = (P("groups", "row"), P("groups", "row"))
    return jax.shard_map(
        functools.partial(on_device, mesh.shape["row"]),
        mesh=mesh,
        in_specs=in_specs,
        out_specs=out_specs,
        check_vma=False,
    )
```

```python
import functools

import jax
import jax.numpy as jnp
from jax import lax
from jax.experimental import pallas as pl
from jax.experimental.pallas import tpu as pltpu
from jax.sharding import PartitionSpec as P

F32 = jnp.float32
BF16 = jnp.bfloat16
LANES = 128
VMEM = pl.BlockSpec(memory_space=pltpu.VMEM)


def lane_sums(cells):
    rows, columns = cells.shape
    width = min(columns, LANES)
    folded = cells[:, 0:width]
    for start in range(width, columns, width):
        folded = folded + cells[:, start : start + width]
    return jnp.sum(folded.T, axis=0, keepdims=True)


def prep_kernel(*refs):
    sources, (inner_out, outer_out, own_out, weight_out), held, done = refs[:7], refs[7:11], refs[11:17], refs[17]
    targets = (*held, weight_out)
    copies = [pltpu.make_async_copy(s, t, done.at[i]) for i, (s, t) in enumerate(zip(sources, targets))]
    for copy in copies:
        copy.start()
    for copy in copies[:-1]:
        copy.wait()
    coeff, status, bit, lower, upper, bias = held
    examples, specs, neurons = coeff.shape
    low, high = lower[...], upper[...]
    slope = high / (high - low)
    unstable = status[...] == 2
    active = status[...] == 1
    inner = jnp.where(active, 1.0, jnp.where(unstable, bit[...].astype(F32), 0.0))
    outer = jnp.where(active, 1.0, jnp.where(unstable, slope, 0.0))
    offset = jnp.where(unstable, -slope * low, 0.0)
    biases = bias[...]
    below, above = [], []
    for e in range(examples):
        inner_rows = jnp.broadcast_to(inner[e : e + 1], (specs, neurons))
        outer_rows = jnp.broadcast_to(outer[e : e + 1], (specs, neurons))
        inner_out[e * specs : (e + 1) * specs, :] = inner_rows
        outer_out[e * specs : (e + 1) * specs, :] = outer_rows
        values = coeff[e].astype(F32)
        positive = values >= 0.0
        relaxed_low = (values * jnp.where(positive, inner_rows, outer_rows)).astype(BF16).astype(F32)
        relaxed_up = (values * jnp.where(positive, outer_rows, inner_rows)).astype(BF16).astype(F32)
        term = values * offset[e : e + 1]
        below.append(jnp.where(positive, 0.0, term) + relaxed_low * biases)
        above.append(jnp.where(positive, term, 0.0) + relaxed_up * biases)
    cells = jnp.concatenate(below + above, axis=0)
    rows = cells.shape[0]
    folded = cells[:, 0:LANES]
    for start in range(LANES, neurons, LANES):
        folded = folded + cells[:, start : start + LANES]
    if rows < LANES:
        folded = jnp.concatenate([folded, jnp.zeros((LANES - rows, LANES), F32)], axis=0)
    own_out[...] = jnp.sum(folded.T, axis=0, keepdims=True)[:, 0:rows]
    copies[-1].wait()


def prep(coeff, status, bit, lower, upper, bias, weight):
    examples, specs, neurons = coeff.shape
    rows = examples * specs
    small = (coeff, status, bit, lower, upper, bias)
    return pl.pallas_call(
        prep_kernel,
        in_specs=[pl.BlockSpec(memory_space=pltpu.HBM)] * 7,
        out_specs=(VMEM, VMEM, VMEM, VMEM),
        out_shape=(
            jax.ShapeDtypeStruct((rows, neurons), F32),
            jax.ShapeDtypeStruct((rows, neurons), F32),
            jax.ShapeDtypeStruct((1, 2 * rows), F32),
            jax.ShapeDtypeStruct(weight.shape, weight.dtype),
        ),
        scratch_shapes=[pltpu.VMEM(a.shape, a.dtype) for a in small] + [pltpu.SemaphoreType.DMA((7,))],
        compiler_params=pltpu.CompilerParams(vmem_limit_bytes=8 << 20),
        cost_estimate=pl.CostEstimate(
            flops=20 * rows * neurons, bytes_accessed=2 * weight.size + 12 * rows * neurons, transcendentals=0
        ),
        name="prep",
    )(*[pltpu.with_memory_space_constraint(a, pltpu.HBM) for a in (*small, weight)])


def map_kernel(num_pieces, *refs):
    pieces = refs[:num_pieces]
    inner, outer, weight, center, radius, out, relaxed = refs[num_pieces:]
    examples, specs, neurons = pieces[0].shape
    rows = examples * specs
    columns = weight.shape[1]
    step = min(neurons, 2048)
    for start in range(0, neurons, step):
        span = slice(start, start + step)
        inner_rows, outer_rows = inner[:, span], outer[:, span]
        for index, piece in enumerate(pieces):
            values = jnp.concatenate([piece[e, :, span].astype(F32) for e in range(examples)], axis=0)
            positive = values >= 0.0
            low = (values * jnp.where(positive, inner_rows, outer_rows)).astype(BF16)
            up = (values * jnp.where(positive, outer_rows, inner_rows)).astype(BF16)
            at = index * 2 * rows
            relaxed[at : at + 2 * rows, span] = jnp.concatenate([low, up], axis=0)
    mapped = jnp.dot(relaxed[...], weight[...], preferred_element_type=F32)
    centers, radii = center[...], radius[...]

    def per_row(values_low, values_up):
        halves = []
        for values in (values_low, values_up):
            for e in range(examples):
                halves.append(jnp.broadcast_to(values[e : e + 1], (specs, columns)))
        block = jnp.concatenate(halves, axis=0)[None]
        return jnp.broadcast_to(block, (num_pieces, 2 * rows, columns)).reshape(num_pieces * 2 * rows, columns)

    cells = mapped * per_row(centers, centers) + jnp.abs(mapped) * per_row(-radii, radii)
    out[...] = lane_sums(cells)


def join_kernel(order, num_pieces, *refs):
    *ins, early, keep_out, send_out, relaxed, late = refs
    map_kernel(num_pieces, *ins, late, relaxed)
    width = early.shape[1] // (len(order) - num_pieces)
    parts = []
    for source, index in order:
        parts.append((early, late)[source][:, index * width : (index + 1) * width])
    half = len(parts) // 2
    keep_out[...] = jnp.concatenate(parts[:half], axis=1)
    send_out[...] = jnp.concatenate(parts[half:], axis=1)


def map_rows(pieces, args, early=None, order=None):
    examples, specs, neurons = pieces[0].shape
    rows = 2 * examples * specs * len(pieces)
    columns = args[2].shape[1]
    scratch = [pltpu.VMEM((rows, neurons), BF16)]
    if early is None:
        kernel, more = functools.partial(map_kernel, len(pieces)), ()
        out_specs, out_shape = VMEM, jax.ShapeDtypeStruct((1, rows), F32)
    else:
        kernel, more = functools.partial(join_kernel, order, len(pieces)), (early,)
        half = (rows + early.shape[1]) // 2
        out_specs, out_shape = (VMEM, VMEM), (jax.ShapeDtypeStruct((1, half), F32),) * 2
        scratch.append(pltpu.VMEM((1, rows), F32))
    return pl.pallas_call(
        kernel,
        in_specs=[VMEM] * (len(pieces) + len(args) + len(more)),
        out_specs=out_specs,
        out_shape=out_shape,
        scratch_shapes=scratch,
        compiler_params=pltpu.CompilerParams(vmem_limit_bytes=24 << 20),
        cost_estimate=pl.CostEstimate(
            flops=2 * rows * neurons * columns, bytes_accessed=2 * rows * neurons, transcendentals=0
        ),
        name="map_rows",
    )(*pieces, *args, *more)


def fold_kernel(kept, came, keep_out, send_out):
    total = kept[...] + came[...]
    half = total.shape[1] // 2
    keep_out[...] = total[:, 0:half]
    send_out[...] = total[:, half:]


def fold(kept, came):
    half = kept.shape[1] // 2
    return pl.pallas_call(
        fold_kernel,
        in_specs=[VMEM] * 2,
        out_specs=(VMEM, VMEM),
        out_shape=(jax.ShapeDtypeStruct((1, half), F32),) * 2,
        compiler_params=pltpu.CompilerParams(vmem_limit_bytes=1 << 20),
        name="fold",
    )(kept, came)


def finish_kernel(kept, came, own, lower_out, upper_out):
    total = kept[...] + came[...] + own[...]
    examples, specs = lower_out.shape
    for e in range(examples):
        lower_out[e : e + 1, :] = total[:, e * specs : (e + 1) * specs]
        at = (examples + e) * specs
        upper_out[e : e + 1, :] = total[:, at : at + specs]


def finish(kept, came, own, examples, specs):
    return pl.pallas_call(
        finish_kernel,
        in_specs=[VMEM] * 3,
        out_specs=(VMEM, VMEM),
        out_shape=(jax.ShapeDtypeStruct((examples, specs), F32),) * 2,
        compiler_params=pltpu.CompilerParams(vmem_limit_bytes=1 << 20),
        name="finish",
    )(kept, came, own)


def on_device(
    num_devices, bound_coeff, status, slope_bit, pre_lower, pre_upper, weight, layer_bias, center_input, radius
):
    examples, specs, neurons = bound_coeff.shape

    def swap(array, mask):
        return lax.ppermute(array, "row", [(i, i ^ mask) for i in range(num_devices)])

    inner, outer, own, held = prep(
        bound_coeff, status, slope_bit, pre_lower, pre_upper, layer_bias.reshape(1, neurons), weight
    )

    bits = num_devices.bit_length() - 1
    far = sorted(range(4, num_devices, 4), key=lambda m: (m.bit_count(), -m))
    direct = [m for m in far if m.bit_count() == 1]
    relayed = [m for m in far if m not in direct]
    pieces = {0: bound_coeff}
    for mask in (*direct, 2):
        pieces[mask] = swap(bound_coeff, mask)
    args = (inner, outer, held, center_input, radius)
    pieces[direct[0]], args = lax.optimization_barrier((pieces[direct[0]], args))
    for mask in relayed:
        low = mask & -mask
        pieces[mask] = swap(pieces[mask ^ low], low)
    for mask in direct[:-1]:
        pieces[mask + 2] = swap(pieces[mask], 2)
    pieces[6] = swap(pieces[2], 4)
    early = [0, *direct, 2]
    first = map_rows([pieces[m] for m in early], args)
    pieces[relayed[-1]], first = lax.optimization_barrier((pieces[relayed[-1]], first))
    for mask in relayed:
        pieces[mask + 2] = swap(pieces[mask], 2)
    others = [*relayed, *[m + 2 for m in direct[:-1]], 6, *[m + 2 for m in relayed]]
    for mask in (*early, *others):
        pieces[mask + 1] = swap(pieces[mask], 1)
    late = [*others, *[m + 1 for m in early], *[m + 1 for m in others]]

    sent = [int(format(i, "b").zfill(bits)[::-1], 2) for i in range(num_devices)]
    order = [(0, early.index(m)) if m in early else (1, late.index(m)) for m in sent]
    keep, send = map_rows([pieces[m] for m in late], args, first, order)
    for bit in range(bits):
        came = swap(send, 1 << bit)
        if bit < bits - 1:
            keep, send = fold(keep, came)
    return finish(keep, came, own, examples, specs)


def solution(mesh):
    in_specs = (
        P("groups", "row", None),
        P("groups", None),
        P("groups", None),
        P("groups", None),
        P("groups", None),
        P("groups", "row"),
        P("groups"),
        P("groups", "row"),
        P("groups", "row"),
    )
    out_specs = (P("groups", "row"), P("groups", "row"))
    return jax.shard_map(
        functools.partial(on_device, mesh.shape["row"]),
        mesh=mesh,
        in_specs=in_specs,
        out_specs=out_specs,
        check_vma=False,
    )
```

```python
import functools

import jax
import jax.numpy as jnp
from jax import lax
from jax.experimental import pallas as pl
from jax.experimental.pallas import tpu as pltpu
from jax.sharding import PartitionSpec as P

F32 = jnp.float32
BF16 = jnp.bfloat16
LANES = 128
VMEM = pl.BlockSpec(memory_space=pltpu.VMEM)


def lane_sums(cells):
    rows, columns = cells.shape
    width = min(columns, LANES)
    folded = cells[:, 0:width]
    for start in range(width, columns, width):
        folded = folded + cells[:, start : start + width]
    return jnp.sum(folded.T, axis=0, keepdims=True)


def prep_kernel(*refs):
    sources, (inner_out, outer_out, own_out, weight_out), held, done = refs[:7], refs[7:11], refs[11:17], refs[17]
    weight = sources[-1]
    chunks = done.shape[0] - len(held)
    step = weight.shape[0] // chunks
    spans = [pl.ds(i * step, step) for i in range(chunks)]
    pairs = [*zip(sources, held), *[(weight.at[span], weight_out.at[span]) for span in spans]]
    copies = [pltpu.make_async_copy(s, t, done.at[i]) for i, (s, t) in enumerate(pairs)]
    for copy in copies:
        copy.start()
    for copy in copies[: len(held)]:
        copy.wait()
    coeff, status, bit, lower, upper, bias = held
    examples, specs, neurons = coeff.shape
    low, high = lower[...], upper[...]
    slope = high / (high - low)
    unstable = status[...] == 2
    active = status[...] == 1
    inner = jnp.where(active, 1.0, jnp.where(unstable, bit[...].astype(F32), 0.0))
    outer = jnp.where(active, 1.0, jnp.where(unstable, slope, 0.0))
    offset = jnp.where(unstable, -slope * low, 0.0)
    biases = bias[...]
    below, above = [], []
    for e in range(examples):
        inner_rows = jnp.broadcast_to(inner[e : e + 1], (specs, neurons))
        outer_rows = jnp.broadcast_to(outer[e : e + 1], (specs, neurons))
        inner_out[e * specs : (e + 1) * specs, :] = inner_rows
        outer_out[e * specs : (e + 1) * specs, :] = outer_rows
        values = coeff[e].astype(F32)
        positive = values >= 0.0
        relaxed_low = (values * jnp.where(positive, inner_rows, outer_rows)).astype(BF16).astype(F32)
        relaxed_up = (values * jnp.where(positive, outer_rows, inner_rows)).astype(BF16).astype(F32)
        term = values * offset[e : e + 1]
        below.append(jnp.where(positive, 0.0, term) + relaxed_low * biases)
        above.append(jnp.where(positive, term, 0.0) + relaxed_up * biases)
    cells = jnp.concatenate(below + above, axis=0)
    rows = cells.shape[0]
    folded = cells[:, 0:LANES]
    for start in range(LANES, neurons, LANES):
        folded = folded + cells[:, start : start + LANES]
    if rows < LANES:
        folded = jnp.concatenate([folded, jnp.zeros((LANES - rows, LANES), F32)], axis=0)
    own_out[...] = jnp.sum(folded.T, axis=0, keepdims=True)[:, 0:rows]
    for copy in copies[len(held) :]:
        copy.wait()


def prep(coeff, status, bit, lower, upper, bias, weight):
    examples, specs, neurons = coeff.shape
    rows = examples * specs
    small = (coeff, status, bit, lower, upper, bias)
    return pl.pallas_call(
        prep_kernel,
        in_specs=[pl.BlockSpec(memory_space=pltpu.HBM)] * 7,
        out_specs=(VMEM, VMEM, VMEM, VMEM),
        out_shape=(
            jax.ShapeDtypeStruct((rows, neurons), F32),
            jax.ShapeDtypeStruct((rows, neurons), F32),
            jax.ShapeDtypeStruct((1, 2 * rows), F32),
            jax.ShapeDtypeStruct(weight.shape, weight.dtype),
        ),
        scratch_shapes=[pltpu.VMEM(a.shape, a.dtype) for a in small] + [pltpu.SemaphoreType.DMA((10,))],
        compiler_params=pltpu.CompilerParams(vmem_limit_bytes=8 << 20),
        cost_estimate=pl.CostEstimate(
            flops=20 * rows * neurons, bytes_accessed=2 * weight.size + 12 * rows * neurons, transcendentals=0
        ),
        name="prep",
    )(*[pltpu.with_memory_space_constraint(a, pltpu.HBM) for a in (*small, weight)])


def map_kernel(num_pieces, *refs):
    pieces = refs[:num_pieces]
    inner, outer, weight, center, radius, out, relaxed = refs[num_pieces:]
    examples, specs, neurons = pieces[0].shape
    rows = examples * specs
    columns = weight.shape[1]
    step = min(neurons, 2048)
    for start in range(0, neurons, step):
        span = slice(start, start + step)
        inner_rows, outer_rows = inner[:, span], outer[:, span]
        for index, piece in enumerate(pieces):
            values = jnp.concatenate([piece[e, :, span].astype(F32) for e in range(examples)], axis=0)
            positive = values >= 0.0
            low = (values * jnp.where(positive, inner_rows, outer_rows)).astype(BF16)
            up = (values * jnp.where(positive, outer_rows, inner_rows)).astype(BF16)
            at = index * 2 * rows
            relaxed[at : at + 2 * rows, span] = jnp.concatenate([low, up], axis=0)
    mapped = jnp.dot(relaxed[...], weight[...], preferred_element_type=F32)
    centers, radii = center[...], radius[...]

    def per_row(values_low, values_up):
        halves = []
        for values in (values_low, values_up):
            for e in range(examples):
                halves.append(jnp.broadcast_to(values[e : e + 1], (specs, columns)))
        block = jnp.concatenate(halves, axis=0)[None]
        return jnp.broadcast_to(block, (num_pieces, 2 * rows, columns)).reshape(num_pieces * 2 * rows, columns)

    cells = mapped * per_row(centers, centers) + jnp.abs(mapped) * per_row(-radii, radii)
    out[...] = lane_sums(cells)


def join_kernel(order, num_pieces, *refs):
    *ins, early, keep_out, send_out, relaxed, late = refs
    map_kernel(num_pieces, *ins, late, relaxed)
    width = early.shape[1] // (len(order) - num_pieces)
    parts = []
    for source, index in order:
        parts.append((early, late)[source][:, index * width : (index + 1) * width])
    half = len(parts) // 2
    keep_out[...] = jnp.concatenate(parts[:half], axis=1)
    send_out[...] = jnp.concatenate(parts[half:], axis=1)


def map_rows(pieces, args, early=None, order=None):
    examples, specs, neurons = pieces[0].shape
    rows = 2 * examples * specs * len(pieces)
    columns = args[2].shape[1]
    scratch = [pltpu.VMEM((rows, neurons), BF16)]
    if early is None:
        kernel, more = functools.partial(map_kernel, len(pieces)), ()
        out_specs, out_shape = VMEM, jax.ShapeDtypeStruct((1, rows), F32)
    else:
        kernel, more = functools.partial(join_kernel, order, len(pieces)), (early,)
        half = (rows + early.shape[1]) // 2
        out_specs, out_shape = (VMEM, VMEM), (jax.ShapeDtypeStruct((1, half), F32),) * 2
        scratch.append(pltpu.VMEM((1, rows), F32))
    return pl.pallas_call(
        kernel,
        in_specs=[VMEM] * (len(pieces) + len(args) + len(more)),
        out_specs=out_specs,
        out_shape=out_shape,
        scratch_shapes=scratch,
        compiler_params=pltpu.CompilerParams(vmem_limit_bytes=24 << 20),
        cost_estimate=pl.CostEstimate(
            flops=2 * rows * neurons * columns, bytes_accessed=2 * rows * neurons, transcendentals=0
        ),
        name="map_rows",
    )(*pieces, *args, *more)


def fold_kernel(kept, came, keep_out, send_out):
    total = kept[...] + came[...]
    half = total.shape[1] // 2
    keep_out[...] = total[:, 0:half]
    send_out[...] = total[:, half:]


def fold(kept, came):
    half = kept.shape[1] // 2
    return pl.pallas_call(
        fold_kernel,
        in_specs=[VMEM] * 2,
        out_specs=(VMEM, VMEM),
        out_shape=(jax.ShapeDtypeStruct((1, half), F32),) * 2,
        compiler_params=pltpu.CompilerParams(vmem_limit_bytes=1 << 20),
        name="fold",
    )(kept, came)


def finish_kernel(kept, came, own, lower_out, upper_out):
    total = kept[...] + came[...] + own[...]
    examples, specs = lower_out.shape
    for e in range(examples):
        lower_out[e : e + 1, :] = total[:, e * specs : (e + 1) * specs]
        at = (examples + e) * specs
        upper_out[e : e + 1, :] = total[:, at : at + specs]


def finish(kept, came, own, examples, specs):
    return pl.pallas_call(
        finish_kernel,
        in_specs=[VMEM] * 3,
        out_specs=(VMEM, VMEM),
        out_shape=(jax.ShapeDtypeStruct((examples, specs), F32),) * 2,
        compiler_params=pltpu.CompilerParams(vmem_limit_bytes=1 << 20),
        name="finish",
    )(kept, came, own)


def on_device(
    num_devices, bound_coeff, status, slope_bit, pre_lower, pre_upper, weight, layer_bias, center_input, radius
):
    examples, specs, neurons = bound_coeff.shape

    def swap(array, mask):
        return lax.ppermute(array, "row", [(i, i ^ mask) for i in range(num_devices)])

    inner, outer, own, held = prep(
        bound_coeff, status, slope_bit, pre_lower, pre_upper, layer_bias.reshape(1, neurons), weight
    )

    bits = num_devices.bit_length() - 1
    highs = sorted(range(8, num_devices, 8), key=lambda m: (m.bit_count(), -m))
    pieces = {0: bound_coeff}
    for high in highs:
        low = high & -high
        pieces[high] = swap(pieces[high ^ low], low)
    for mask in (4, 2, 6):
        pieces[mask] = swap(bound_coeff, mask)
    args = (inner, outer, held, center_input, radius)
    pieces[8], args = lax.optimization_barrier((pieces[8], args))
    for high in highs:
        for mask in (6, 4, 2):
            pieces[high + mask] = swap(pieces[high], mask)
    early = [0, 8, 4, 2, 6]
    for mask in early:
        if mask & 1 and mask not in pieces:
            pieces[mask] = swap(pieces[mask - 1], 1)
    first = map_rows([pieces[m] for m in early], args)
    pieces[highs[-1] + 6], first = lax.optimization_barrier((pieces[highs[-1] + 6], first))
    for mask in range(0, num_devices, 2):
        if mask + 1 not in pieces:
            pieces[mask + 1] = swap(pieces[mask], 1)
    late = sorted([m for m in range(num_devices) if m not in early], key=lambda m: (m & 1, -(m & 8), -(m & 6)))

    sent = [int(format(i, "b").zfill(bits)[::-1], 2) for i in range(num_devices)]
    order = [(0, early.index(m)) if m in early else (1, late.index(m)) for m in sent]
    keep, send = map_rows([pieces[m] for m in late], args, first, order)
    for bit in range(bits):
        came = swap(send, 1 << bit)
        if bit < bits - 1:
            keep, send = fold(keep, came)
    return finish(keep, came, own, examples, specs)


def solution(mesh):
    in_specs = (
        P("groups", "row", None),
        P("groups", None),
        P("groups", None),
        P("groups", None),
        P("groups", None),
        P("groups", "row"),
        P("groups"),
        P("groups", "row"),
        P("groups", "row"),
    )
    out_specs = (P("groups", "row"), P("groups", "row"))
    return jax.shard_map(
        functools.partial(on_device, mesh.shape["row"]),
        mesh=mesh,
        in_specs=in_specs,
        out_specs=out_specs,
        check_vma=False,
    )
```

```python
import functools

import jax
import jax.numpy as jnp
from jax import lax
from jax.experimental import pallas as pl
from jax.experimental.pallas import tpu as pltpu
from jax.sharding import PartitionSpec as P

F32 = jnp.float32
BF16 = jnp.bfloat16
LANES = 128
VMEM = pl.BlockSpec(memory_space=pltpu.VMEM)


def lane_sums(cells):
    rows, columns = cells.shape
    width = min(columns, LANES)
    folded = cells[:, 0:width]
    for start in range(width, columns, width):
        folded = folded + cells[:, start : start + width]
    return jnp.sum(folded.T, axis=0, keepdims=True)


def prep_kernel(*refs):
    sources, (inner_out, outer_out, own_out, weight_out), held, done = refs[:7], refs[7:11], refs[11:17], refs[17]
    weight = sources[-1]
    chunks = done.shape[0] - len(held)
    step = weight.shape[0] // chunks
    spans = [pl.ds(i * step, step) for i in range(chunks)]
    pairs = [*zip(sources, held), *[(weight.at[span], weight_out.at[span]) for span in spans]]
    copies = [pltpu.make_async_copy(s, t, done.at[i]) for i, (s, t) in enumerate(pairs)]
    for copy in copies:
        copy.start()
    for copy in copies[: len(held)]:
        copy.wait()
    coeff, status, bit, lower, upper, bias = held
    examples, specs, neurons = coeff.shape
    low, high = lower[...], upper[...]
    slope = high / (high - low)
    unstable = status[...] == 2
    active = status[...] == 1
    inner = jnp.where(active, 1.0, jnp.where(unstable, bit[...].astype(F32), 0.0))
    outer = jnp.where(active, 1.0, jnp.where(unstable, slope, 0.0))
    offset = jnp.where(unstable, -slope * low, 0.0)
    biases = bias[...]
    below, above = [], []
    for e in range(examples):
        inner_rows = jnp.broadcast_to(inner[e : e + 1], (specs, neurons))
        outer_rows = jnp.broadcast_to(outer[e : e + 1], (specs, neurons))
        inner_out[e * specs : (e + 1) * specs, :] = inner_rows
        outer_out[e * specs : (e + 1) * specs, :] = outer_rows
        values = coeff[e].astype(F32)
        positive = values >= 0.0
        relaxed_low = (values * jnp.where(positive, inner_rows, outer_rows)).astype(BF16).astype(F32)
        relaxed_up = (values * jnp.where(positive, outer_rows, inner_rows)).astype(BF16).astype(F32)
        term = values * offset[e : e + 1]
        below.append(jnp.where(positive, 0.0, term) + relaxed_low * biases)
        above.append(jnp.where(positive, term, 0.0) + relaxed_up * biases)
    cells = jnp.concatenate(below + above, axis=0)
    rows = cells.shape[0]
    folded = cells[:, 0:LANES]
    for start in range(LANES, neurons, LANES):
        folded = folded + cells[:, start : start + LANES]
    if rows < LANES:
        folded = jnp.concatenate([folded, jnp.zeros((LANES - rows, LANES), F32)], axis=0)
    own_out[...] = jnp.sum(folded.T, axis=0, keepdims=True)[:, 0:rows]
    for copy in copies[len(held) :]:
        copy.wait()


def prep(coeff, status, bit, lower, upper, bias, weight):
    examples, specs, neurons = coeff.shape
    rows = examples * specs
    small = (coeff, status, bit, lower, upper, bias)
    return pl.pallas_call(
        prep_kernel,
        in_specs=[pl.BlockSpec(memory_space=pltpu.HBM)] * 7,
        out_specs=(VMEM, VMEM, VMEM, VMEM),
        out_shape=(
            jax.ShapeDtypeStruct((rows, neurons), F32),
            jax.ShapeDtypeStruct((rows, neurons), F32),
            jax.ShapeDtypeStruct((1, 2 * rows), F32),
            jax.ShapeDtypeStruct(weight.shape, weight.dtype),
        ),
        scratch_shapes=[pltpu.VMEM(a.shape, a.dtype) for a in small] + [pltpu.SemaphoreType.DMA((10,))],
        compiler_params=pltpu.CompilerParams(vmem_limit_bytes=8 << 20),
        cost_estimate=pl.CostEstimate(
            flops=20 * rows * neurons, bytes_accessed=2 * weight.size + 12 * rows * neurons, transcendentals=0
        ),
        name="prep",
    )(*[pltpu.with_memory_space_constraint(a, pltpu.HBM) for a in (*small, weight)])


def map_kernel(num_pieces, *refs):
    pieces = refs[:num_pieces]
    inner, outer, weight, center, radius, out, relaxed = refs[num_pieces:]
    examples, specs, neurons = pieces[0].shape
    rows = examples * specs
    columns = weight.shape[1]
    step = min(neurons, 1024)
    for start in range(0, neurons, step):
        span = slice(start, start + step)
        inner_rows, outer_rows = inner[:, span], outer[:, span]
        for index, piece in enumerate(pieces):
            values = jnp.concatenate([piece[e, :, span].astype(F32) for e in range(examples)], axis=0)
            positive = values >= 0.0
            low = (values * jnp.where(positive, inner_rows, outer_rows)).astype(BF16)
            up = (values * jnp.where(positive, outer_rows, inner_rows)).astype(BF16)
            at = index * 2 * rows
            relaxed[at : at + 2 * rows, span] = jnp.concatenate([low, up], axis=0)
        term = jnp.dot(relaxed[:, span], weight[span, :], preferred_element_type=F32)
        mapped = term if start == 0 else mapped + term
    centers, radii = center[...], radius[...]

    def per_row(values_low, values_up):
        halves = []
        for values in (values_low, values_up):
            for e in range(examples):
                halves.append(jnp.broadcast_to(values[e : e + 1], (specs, columns)))
        block = jnp.concatenate(halves, axis=0)[None]
        return jnp.broadcast_to(block, (num_pieces, 2 * rows, columns)).reshape(num_pieces * 2 * rows, columns)

    cells = mapped * per_row(centers, centers) + jnp.abs(mapped) * per_row(-radii, radii)
    out[...] = lane_sums(cells)


def join_kernel(order, num_pieces, *refs):
    *ins, early, keep_out, send_out, relaxed, late = refs
    map_kernel(num_pieces, *ins, late, relaxed)
    width = early.shape[1] // (len(order) - num_pieces)
    parts = []
    for source, index in order:
        parts.append((early, late)[source][:, index * width : (index + 1) * width])
    half = len(parts) // 2
    keep_out[...] = jnp.concatenate(parts[:half], axis=1)
    send_out[...] = jnp.concatenate(parts[half:], axis=1)


def map_rows(pieces, args, early=None, order=None):
    examples, specs, neurons = pieces[0].shape
    rows = 2 * examples * specs * len(pieces)
    columns = args[2].shape[1]
    scratch = [pltpu.VMEM((rows, neurons), BF16)]
    if early is None:
        kernel, more = functools.partial(map_kernel, len(pieces)), ()
        out_specs, out_shape = VMEM, jax.ShapeDtypeStruct((1, rows), F32)
    else:
        kernel, more = functools.partial(join_kernel, order, len(pieces)), (early,)
        half = (rows + early.shape[1]) // 2
        out_specs, out_shape = (VMEM, VMEM), (jax.ShapeDtypeStruct((1, half), F32),) * 2
        scratch.append(pltpu.VMEM((1, rows), F32))
    return pl.pallas_call(
        kernel,
        in_specs=[VMEM] * (len(pieces) + len(args) + len(more)),
        out_specs=out_specs,
        out_shape=out_shape,
        scratch_shapes=scratch,
        compiler_params=pltpu.CompilerParams(vmem_limit_bytes=24 << 20),
        cost_estimate=pl.CostEstimate(
            flops=2 * rows * neurons * columns, bytes_accessed=2 * rows * neurons, transcendentals=0
        ),
        name="map_rows",
    )(*pieces, *args, *more)


def fold_kernel(kept, came, keep_out, send_out):
    total = kept[...] + came[...]
    half = total.shape[1] // 2
    keep_out[...] = total[:, 0:half]
    send_out[...] = total[:, half:]


def fold(kept, came):
    half = kept.shape[1] // 2
    return pl.pallas_call(
        fold_kernel,
        in_specs=[VMEM] * 2,
        out_specs=(VMEM, VMEM),
        out_shape=(jax.ShapeDtypeStruct((1, half), F32),) * 2,
        compiler_params=pltpu.CompilerParams(vmem_limit_bytes=1 << 20),
        name="fold",
    )(kept, came)


def finish_kernel(kept, came, own, lower_out, upper_out):
    total = kept[...] + came[...] + own[...]
    examples, specs = lower_out.shape
    for e in range(examples):
        lower_out[e : e + 1, :] = total[:, e * specs : (e + 1) * specs]
        at = (examples + e) * specs
        upper_out[e : e + 1, :] = total[:, at : at + specs]


def finish(kept, came, own, examples, specs):
    return pl.pallas_call(
        finish_kernel,
        in_specs=[VMEM] * 3,
        out_specs=(VMEM, VMEM),
        out_shape=(jax.ShapeDtypeStruct((examples, specs), F32),) * 2,
        compiler_params=pltpu.CompilerParams(vmem_limit_bytes=1 << 20),
        name="finish",
    )(kept, came, own)


def on_device(
    num_devices, bound_coeff, status, slope_bit, pre_lower, pre_upper, weight, layer_bias, center_input, radius
):
    examples, specs, neurons = bound_coeff.shape

    def swap(array, mask):
        return lax.ppermute(array, "row", [(i, i ^ mask) for i in range(num_devices)])

    inner, outer, own, held = prep(
        bound_coeff, status, slope_bit, pre_lower, pre_upper, layer_bias.reshape(1, neurons), weight
    )

    bits = num_devices.bit_length() - 1
    highs = sorted(range(8, num_devices, 8), key=lambda m: (m.bit_count(), -m))
    pieces = {0: bound_coeff}
    for high in highs:
        low = high & -high
        pieces[high] = swap(pieces[high ^ low], low)
    for mask in (4, 2, 6):
        pieces[mask] = swap(bound_coeff, mask)
    args = (inner, outer, held, center_input, radius)
    pieces[8], args = lax.optimization_barrier((pieces[8], args))
    pieces[6], args = lax.optimization_barrier((pieces[6], args))
    for high in highs:
        for mask in (6, 4, 2):
            pieces[high + mask] = swap(pieces[high], mask)
    early = [0, 8, 4, 2, 6]
    for mask in early:
        if mask & 1 and mask not in pieces:
            pieces[mask] = swap(pieces[mask - 1], 1)
    first = map_rows([pieces[m] for m in early], args)
    pieces[highs[-1] + 6], first = lax.optimization_barrier((pieces[highs[-1] + 6], first))
    for mask in range(0, num_devices, 2):
        if mask + 1 not in pieces:
            pieces[mask + 1] = swap(pieces[mask], 1)
    late = sorted([m for m in range(num_devices) if m not in early], key=lambda m: (m & 1, -(m & 8), -(m & 6)))

    sent = [int(format(i, "b").zfill(bits)[::-1], 2) for i in range(num_devices)]
    order = [(0, early.index(m)) if m in early else (1, late.index(m)) for m in sent]
    keep, send = map_rows([pieces[m] for m in late], args, first, order)
    for bit in range(bits):
        came = swap(send, 1 << bit)
        if bit < bits - 1:
            keep, send = fold(keep, came)
    return finish(keep, came, own, examples, specs)


def solution(mesh):
    in_specs = (
        P("groups", "row", None),
        P("groups", None),
        P("groups", None),
        P("groups", None),
        P("groups", None),
        P("groups", "row"),
        P("groups"),
        P("groups", "row"),
        P("groups", "row"),
    )
    out_specs = (P("groups", "row"), P("groups", "row"))
    return jax.shard_map(
        functools.partial(on_device, mesh.shape["row"]),
        mesh=mesh,
        in_specs=in_specs,
        out_specs=out_specs,
        check_vma=False,
    )
```

```python
import functools

import jax
import jax.numpy as jnp
from jax import lax
from jax.experimental import pallas as pl
from jax.experimental.pallas import tpu as pltpu
from jax.sharding import PartitionSpec as P

F32 = jnp.float32
BF16 = jnp.bfloat16
LANES = 128
VMEM = pl.BlockSpec(memory_space=pltpu.VMEM)


def lane_sums(cells):
    rows, columns = cells.shape
    width = min(columns, LANES)
    folded = cells[:, 0:width]
    for start in range(width, columns, width):
        folded = folded + cells[:, start : start + width]
    return jnp.sum(folded.T, axis=0, keepdims=True)


def prep_kernel(*refs):
    sources, (inner_out, outer_out, own_out, weight_out), held, done = refs[:7], refs[7:11], refs[11:17], refs[17]
    weight = sources[-1]
    chunks = done.shape[0] - len(held)
    step = weight.shape[0] // chunks
    spans = [pl.ds(i * step, step) for i in range(chunks)]
    pairs = [*zip(sources, held), *[(weight.at[span], weight_out.at[span]) for span in spans]]
    copies = [pltpu.make_async_copy(s, t, done.at[i]) for i, (s, t) in enumerate(pairs)]
    for copy in copies:
        copy.start()
    for copy in copies[: len(held)]:
        copy.wait()
    coeff, status, bit, lower, upper, bias = held
    examples, specs, neurons = coeff.shape
    low, high = lower[...], upper[...]
    slope = high / (high - low)
    unstable = status[...] == 2
    active = status[...] == 1
    inner = jnp.where(active, 1.0, jnp.where(unstable, bit[...].astype(F32), 0.0))
    outer = jnp.where(active, 1.0, jnp.where(unstable, slope, 0.0))
    offset = jnp.where(unstable, -slope * low, 0.0)
    biases = bias[...]
    below, above = [], []
    for e in range(examples):
        inner_rows = jnp.broadcast_to(inner[e : e + 1], (specs, neurons))
        outer_rows = jnp.broadcast_to(outer[e : e + 1], (specs, neurons))
        inner_out[e * specs : (e + 1) * specs, :] = inner_rows
        outer_out[e * specs : (e + 1) * specs, :] = outer_rows
        values = coeff[e].astype(F32)
        positive = values >= 0.0
        relaxed_low = (values * jnp.where(positive, inner_rows, outer_rows)).astype(BF16).astype(F32)
        relaxed_up = (values * jnp.where(positive, outer_rows, inner_rows)).astype(BF16).astype(F32)
        term = values * offset[e : e + 1]
        below.append(jnp.where(positive, 0.0, term) + relaxed_low * biases)
        above.append(jnp.where(positive, term, 0.0) + relaxed_up * biases)
    cells = jnp.concatenate(below + above, axis=0)
    rows = cells.shape[0]
    folded = cells[:, 0:LANES]
    for start in range(LANES, neurons, LANES):
        folded = folded + cells[:, start : start + LANES]
    if rows < LANES:
        folded = jnp.concatenate([folded, jnp.zeros((LANES - rows, LANES), F32)], axis=0)
    own_out[...] = jnp.sum(folded.T, axis=0, keepdims=True)[:, 0:rows]
    for copy in copies[len(held) :]:
        copy.wait()


def prep(coeff, status, bit, lower, upper, bias, weight):
    examples, specs, neurons = coeff.shape
    rows = examples * specs
    small = (coeff, status, bit, lower, upper, bias)
    return pl.pallas_call(
        prep_kernel,
        in_specs=[pl.BlockSpec(memory_space=pltpu.HBM)] * 7,
        out_specs=(VMEM, VMEM, VMEM, VMEM),
        out_shape=(
            jax.ShapeDtypeStruct((rows, neurons), F32),
            jax.ShapeDtypeStruct((rows, neurons), F32),
            jax.ShapeDtypeStruct((1, 2 * rows), F32),
            jax.ShapeDtypeStruct(weight.shape, weight.dtype),
        ),
        scratch_shapes=[pltpu.VMEM(a.shape, a.dtype) for a in small] + [pltpu.SemaphoreType.DMA((10,))],
        compiler_params=pltpu.CompilerParams(vmem_limit_bytes=8 << 20),
        cost_estimate=pl.CostEstimate(
            flops=20 * rows * neurons, bytes_accessed=2 * weight.size + 12 * rows * neurons, transcendentals=0
        ),
        name="prep",
    )(*[pltpu.with_memory_space_constraint(a, pltpu.HBM) for a in (*small, weight)])


def map_kernel(num_pieces, *refs):
    pieces = refs[:num_pieces]
    inner, outer, weight, center, radius, out, relaxed = refs[num_pieces:]
    examples, specs, neurons = pieces[0].shape
    rows = examples * specs
    columns = weight.shape[1]
    step = min(neurons, 2048)
    for start in range(0, neurons, step):
        span = slice(start, start + step)
        inner_rows, outer_rows = inner[:, span], outer[:, span]
        for index, piece in enumerate(pieces):
            values = jnp.concatenate([piece[e, :, span].astype(F32) for e in range(examples)], axis=0)
            positive = values >= 0.0
            low = (values * jnp.where(positive, inner_rows, outer_rows)).astype(BF16)
            up = (values * jnp.where(positive, outer_rows, inner_rows)).astype(BF16)
            at = index * 2 * rows
            relaxed[at : at + 2 * rows, span] = jnp.concatenate([low, up], axis=0)
    mapped = jnp.dot(relaxed[...], weight[...], preferred_element_type=F32)
    centers, radii = center[...], radius[...]

    def per_row(values_low, values_up):
        halves = []
        for values in (values_low, values_up):
            for e in range(examples):
                halves.append(jnp.broadcast_to(values[e : e + 1], (specs, columns)))
        block = jnp.concatenate(halves, axis=0)[None]
        return jnp.broadcast_to(block, (num_pieces, 2 * rows, columns)).reshape(num_pieces * 2 * rows, columns)

    cells = mapped * per_row(centers, centers) + jnp.abs(mapped) * per_row(-radii, radii)
    out[...] = lane_sums(cells)


def join_kernel(order, num_pieces, *refs):
    *ins, early, keep_out, send_out, relaxed, late = refs
    map_kernel(num_pieces, *ins, late, relaxed)
    width = early.shape[1] // (len(order) - num_pieces)
    parts = []
    for source, index in order:
        parts.append((early, late)[source][:, index * width : (index + 1) * width])
    half = len(parts) // 2
    keep_out[...] = jnp.concatenate(parts[:half], axis=1)
    send_out[...] = jnp.concatenate(parts[half:], axis=1)


def map_rows(pieces, args, early=None, order=None):
    examples, specs, neurons = pieces[0].shape
    rows = 2 * examples * specs * len(pieces)
    columns = args[2].shape[1]
    scratch = [pltpu.VMEM((rows, neurons), BF16)]
    if early is None:
        kernel, more = functools.partial(map_kernel, len(pieces)), ()
        out_specs, out_shape = VMEM, jax.ShapeDtypeStruct((1, rows), F32)
    else:
        kernel, more = functools.partial(join_kernel, order, len(pieces)), (early,)
        half = (rows + early.shape[1]) // 2
        out_specs, out_shape = (VMEM, VMEM), (jax.ShapeDtypeStruct((1, half), F32),) * 2
        scratch.append(pltpu.VMEM((1, rows), F32))
    return pl.pallas_call(
        kernel,
        in_specs=[VMEM] * (len(pieces) + len(args) + len(more)),
        out_specs=out_specs,
        out_shape=out_shape,
        scratch_shapes=scratch,
        compiler_params=pltpu.CompilerParams(vmem_limit_bytes=24 << 20),
        cost_estimate=pl.CostEstimate(
            flops=2 * rows * neurons * columns, bytes_accessed=2 * rows * neurons, transcendentals=0
        ),
        name="map_rows",
    )(*pieces, *args, *more)


def fold_kernel(kept, came, keep_out, send_out):
    total = kept[...] + came[...]
    half = total.shape[1] // 2
    keep_out[...] = total[:, 0:half]
    send_out[...] = total[:, half:]


def fold(kept, came):
    half = kept.shape[1] // 2
    return pl.pallas_call(
        fold_kernel,
        in_specs=[VMEM] * 2,
        out_specs=(VMEM, VMEM),
        out_shape=(jax.ShapeDtypeStruct((1, half), F32),) * 2,
        compiler_params=pltpu.CompilerParams(vmem_limit_bytes=1 << 20),
        name="fold",
    )(kept, came)


def finish_kernel(kept, came, own, lower_out, upper_out):
    total = kept[...] + came[...] + own[...]
    examples, specs = lower_out.shape
    for e in range(examples):
        lower_out[e : e + 1, :] = total[:, e * specs : (e + 1) * specs]
        at = (examples + e) * specs
        upper_out[e : e + 1, :] = total[:, at : at + specs]


def finish(kept, came, own, examples, specs):
    return pl.pallas_call(
        finish_kernel,
        in_specs=[VMEM] * 3,
        out_specs=(VMEM, VMEM),
        out_shape=(jax.ShapeDtypeStruct((examples, specs), F32),) * 2,
        compiler_params=pltpu.CompilerParams(vmem_limit_bytes=1 << 20),
        name="finish",
    )(kept, came, own)


def on_device(
    num_devices, bound_coeff, status, slope_bit, pre_lower, pre_upper, weight, layer_bias, center_input, radius
):
    examples, specs, neurons = bound_coeff.shape

    def swap(array, mask):
        return lax.ppermute(array, "row", [(i, i ^ mask) for i in range(num_devices)])

    inner, outer, own, held = prep(
        bound_coeff, status, slope_bit, pre_lower, pre_upper, layer_bias.reshape(1, neurons), weight
    )

    bits = num_devices.bit_length() - 1
    highs = sorted(range(8, num_devices, 8), key=lambda m: (m.bit_count(), -m))
    pieces = {0: bound_coeff}
    for high in highs:
        low = high & -high
        pieces[high] = swap(pieces[high ^ low], low)
    for mask in (4, 2, 6):
        pieces[mask] = swap(bound_coeff, mask)
    args = (inner, outer, held, center_input, radius)
    pieces[8], args = lax.optimization_barrier((pieces[8], args))
    for high in highs:
        for mask in (6, 4, 2):
            pieces[high + mask] = swap(pieces[high], mask)
    early = [0, 8, 4, 2, 6]
    for mask in early:
        if mask & 1 and mask not in pieces:
            pieces[mask] = swap(pieces[mask - 1], 1)
    first = map_rows([pieces[m] for m in early], args)
    pieces[highs[-1] + 6], first = lax.optimization_barrier((pieces[highs[-1] + 6], first))
    for mask in (8, 6):
        pieces[mask], first = lax.optimization_barrier((pieces[mask], first))
    for mask in range(0, num_devices, 2):
        if mask + 1 not in pieces:
            pieces[mask + 1] = swap(pieces[mask], 1)
    late = sorted([m for m in range(num_devices) if m not in early], key=lambda m: (m & 1, -(m & 8), -(m & 6)))

    sent = [int(format(i, "b").zfill(bits)[::-1], 2) for i in range(num_devices)]
    order = [(0, early.index(m)) if m in early else (1, late.index(m)) for m in sent]
    keep, send = map_rows([pieces[m] for m in late], args, first, order)
    for bit in range(bits):
        came = swap(send, 1 << bit)
        if bit < bits - 1:
            keep, send = fold(keep, came)
    return finish(keep, came, own, examples, specs)


def solution(mesh):
    in_specs = (
        P("groups", "row", None),
        P("groups", None),
        P("groups", None),
        P("groups", None),
        P("groups", None),
        P("groups", "row"),
        P("groups"),
        P("groups", "row"),
        P("groups", "row"),
    )
    out_specs = (P("groups", "row"), P("groups", "row"))
    return jax.shard_map(
        functools.partial(on_device, mesh.shape["row"]),
        mesh=mesh,
        in_specs=in_specs,
        out_specs=out_specs,
        check_vma=False,
    )
```
